256 devices in a mesh: ctx: 16 (over y, x), req: 16 (over z, core).
Axes of the slice: x: 4, y: 4, z: 8, core: 2. Of those that a mesh axis runs over, the one named last changes fastest.
Arguments:
- queries: bfloat16 [1024, 64, 128], P('req', 'ctx'), may hold values from -96 to 96
- prefix_keys: bfloat16 [32768, 1024], P('ctx'), may hold values from -9 to 9
- lengths: int32 [64], P('req'), may hold values from 4096 to 32768, as said below
- positions: int32 [64, 16], P('req'), may hold values from 2048 to 34816, as said below
- pool_width: int32 [8], replicated, may hold values from 1 to 7, as said below
- scorer_in: bfloat16 [1024, 1024], replicated, may hold values from -0.1875 to 0.1875
- scorer_out: bfloat16 [1024, 8], replicated, may hold values from -0.1875 to 0.1875
Outputs:
- importance: float32 [8, 32768], P(None, ('ctx', 'req'))
The draws below stay inside these ranges and needn't reach their ends.
Inputs may be any that keep to these rules, and one draw needn't show every extreme that they name: `lengths`: some request's length is exactly 32768 and some other's exactly 4096. `positions`: each is 2 or more and lies within 2048 of its request's length. `pool_width`: some key head's width is exactly 7 and some other's exactly 1.
All inputs are finite; a program needn't handle non-finite values.
Results may differ from the reference program's by a relative error of at most 0.0003.
The reference program's roundings to bfloat16 on the way (of `hidden`) count: a program that leaves them out, or rounds other values in their place, can miss the bound.
Values may be sent and summed in bfloat16 or wider, within the bound.
No kernel may reach another device: no remote copies, remote signals or barrier semaphores. Data moves between devices by JAX's collectives and lax.ppermute only.
A program may use at most 64 MiB of HBM per device.

```python
import math
import jax
import jax.numpy as jnp
from jax import lax

HEADS = 64
KVH = 8
HDIM = 128
GROUP = 8
WIN = 16
SHID = 1024
RAD = 3
KEY_DEV = 2048
REQS = 64
KEYS = 32768


def base_keys(key):
    noise_key = jax.random.fold_in(jax.random.fold_in(key, 101), 0)
    values = jax.random.truncated_normal(noise_key, -6.0, 6.0, (KEYS, KVH * HDIM), jnp.float32)
    return values


def draw_prefix_keys(key, part):
    return base_keys(key).astype(jnp.bfloat16)


def draw_queries(key, part):
    noise_key = jax.random.fold_in(jax.random.fold_in(key, 202), 0)
    values = jax.random.truncated_normal(noise_key, -6.0, 6.0, (REQS * WIN, HEADS, HDIM), jnp.float32)
    return values.astype(jnp.bfloat16)


def request_spans(key):
    long_key, modest_key, chance_key, choose_key, jitter_key = jax.random.split(jax.random.fold_in(key, 303), 5)
    modest = jax.random.randint(modest_key, (REQS,), KEYS // 8, KEYS // 2 + 1)
    longer = jax.random.randint(long_key, (REQS,), KEYS // 2, KEYS + 1)
    chance = jax.random.randint(chance_key, (REQS,), 0, 8) == 0
    lengths = jnp.where(chance, longer, modest)
    chosen = jax.random.randint(choose_key, (), 0, REQS)
    shortest = (chosen + 1) % REQS
    request_index = jnp.arange(REQS)
    lengths = jnp.where(request_index == chosen, KEYS, lengths)
    lengths = jnp.where(request_index == shortest, KEYS // 8, lengths)
    jitter = jax.random.randint(jitter_key, (REQS, WIN), -KEY_DEV, KEY_DEV + 1)
    positions = jnp.maximum(lengths[:, None] + jitter, 2)
    window_index = jnp.arange(WIN)
    top_slot = (request_index[:, None] == chosen) & (window_index[None, :] == WIN - 1)
    low_slot = (request_index[:, None] == shortest) & (window_index[None, :] == 0)
    positions = jnp.where(top_slot, KEYS + KEY_DEV, positions)
    positions = jnp.where(low_slot, max(2, KEYS // 8 - KEY_DEV), positions)
    return (lengths.astype(jnp.int32), positions.astype(jnp.int32))


def draw_lengths(key, part):
    return request_spans(key)[0]


def draw_positions(key, part):
    return request_spans(key)[1]


def draw_pool_width(key, part):
    width_key, head_key = jax.random.split(jax.random.fold_in(key, 404))
    widths = jax.random.randint(width_key, (KVH,), 1, 2 * RAD + 2)
    widest = jax.random.randint(head_key, (), 0, KVH)
    narrowest = (widest + 1) % KVH
    head_index = jnp.arange(KVH)
    widths = jnp.where(head_index == widest, 2 * RAD + 1, widths)
    widths = jnp.where(head_index == narrowest, 1, widths)
    return widths.astype(jnp.int32)


def scatter_about(own_key, shape, spread, bound, dtype=jnp.bfloat16):
    return jnp.clip(spread * jax.random.normal(own_key, shape, jnp.float32), -bound, bound).astype(dtype)


def setup_inputs(seed: int = 0) -> dict:
    seeds = jax.random.split(jax.random.key(seed), 8)
    queries = draw_queries(jax.random.fold_in(seeds[7], 71), 0)
    prefix_keys = draw_prefix_keys(jax.random.fold_in(seeds[7], 71), 0)
    lengths = draw_lengths(jax.random.fold_in(seeds[7], 71), 0)
    positions = draw_positions(jax.random.fold_in(seeds[7], 71), 0)
    pool_width = draw_pool_width(jax.random.fold_in(seeds[7], 71), 0)
    scorer_in = scatter_about(seeds[5], (KVH * HDIM, SHID), (KVH * HDIM) ** -0.5, 0.1875)
    scorer_out = scatter_about(seeds[6], (SHID, KVH), SHID ** -0.5, 0.1875)
    return dict(queries=queries, prefix_keys=prefix_keys, lengths=lengths, positions=positions, pool_width=pool_width, scorer_in=scorer_in, scorer_out=scorer_out)


MASKED = -1e+30

def reference(queries, prefix_keys, lengths, positions, pool_width, scorer_in, scorer_out):
    keyed = prefix_keys.reshape(KEYS, KVH, HDIM).astype(jnp.float32)
    key_index = lax.iota(jnp.int32, KEYS)
    limits = jnp.minimum(positions, lengths[:, None] - 1).astype(jnp.int32)
    grouped = queries.reshape(REQS, WIN, KVH, GROUP, HDIM)

    def per_request(totals, inputs):
        query_block, limit_row = inputs
        scores = jnp.einsum('wvgd,kvd->vwgk', query_block.astype(jnp.float32), keyed) * (1.0 / math.sqrt(HDIM))
        visible = key_index[None, :] <= limit_row[:, None]
        scores = jnp.where(visible[None, :, None, :], scores, MASKED)
        highest = lax.optimization_barrier(jnp.max(scores, axis=-1, keepdims=True))
        weights = jnp.exp(scores - highest)
        total = lax.optimization_barrier(jnp.sum(weights, axis=-1, keepdims=True))
        return (totals + lax.optimization_barrier(jnp.sum(weights / total, axis=(1, 2))), None)
    columns = lax.scan(per_request, jnp.zeros((KVH, KEYS), jnp.float32), (grouped, limits))[0]
    padded = jnp.pad(columns, ((0, 0), (RAD, RAD)))
    window_sum = jnp.zeros_like(columns)
    for tap_offset in range(-RAD, RAD + 1):
        inside = (tap_offset >= -(pool_width // 2)) & (tap_offset <= (pool_width - 1) // 2)
        window_sum = window_sum + jnp.where(inside[:, None], padded[:, RAD + tap_offset:RAD + tap_offset + KEYS], 0.0)
    pooled = window_sum / pool_width.astype(jnp.float32)[:, None]
    projected = jnp.dot(prefix_keys.astype(jnp.float32), scorer_in.astype(jnp.float32), precision=lax.Precision.HIGHEST)
    hidden = jax.nn.silu(projected).astype(jnp.bfloat16)
    gating = jnp.dot(hidden.astype(jnp.float32), scorer_out.astype(jnp.float32), precision=lax.Precision.HIGHEST)
    return pooled * (2.0 * jax.nn.sigmoid(gating.T))
```

```python
import math

import jax
import jax.numpy as jnp
from jax import lax
from jax.experimental import pallas as pl
from jax.experimental.pallas import tpu as pltpu
from jax.sharding import PartitionSpec as P

RAD = 3
MASKED = -1e30
LOG2E = 1.4426950408889634
HALO = 128
EDGE = 16
NT = (((1,), (1,)), ((), ()))


def penalty_rows(first_key, count, limits, is_halo, key_total, key_dev):
    local = lax.broadcasted_iota(jnp.int32, (count, 128), 0)
    if is_halo:
        after = local < HALO // 2
        key = jnp.where(after, first_key + key_dev + local, first_key - HALO + local)
        real = ((local < RAD) | (local >= HALO - RAD)) & (key >= 0) & (key < key_total)
        return jnp.where(real & (key <= limits), 0.0, MASKED).astype(jnp.bfloat16)
    return jnp.where(first_key + local <= limits, 0.0, MASKED).astype(jnp.bfloat16)


def one_hot_rows(chunk_rows, heads, row_count):
    row = lax.broadcasted_iota(jnp.int32, (chunk_rows, 128), 0)
    lane = lax.broadcasted_iota(jnp.int32, (chunk_rows, 128), 1)
    low = lane * heads
    return jnp.where((row >= low) & (row < low + heads), 1.0, 0.0).astype(jnp.bfloat16)


def stats_kernel(first_ref, q_ref, k_ref, lim_ref, out_ref, kaug, qaug, lse, *, heads, row_count, scale2):
    v = pl.program_id(0)
    per, chunk_rows, head_dim = q_ref.shape
    key_dev = k_ref.shape[0]
    block = 256

    @pl.when(v == 0)
    def _():
        for b in range(key_dev // block):
            kaug[b * block : (b + 1) * block, head_dim:] = penalty_rows(
                first_ref[0] + b * block, block, lim_ref[...], False, 0, 0
            )
        hot = one_hot_rows(chunk_rows, heads, row_count)
        for p in range(per):
            qaug[p * chunk_rows : (p + 1) * chunk_rows, head_dim:] = hot

    kaug[:, :head_dim] = k_ref[...]
    for p in range(per):
        qaug[p * chunk_rows : (p + 1) * chunk_rows, :head_dim] = q_ref[p]
    for p in range(per):
        s = lax.dot_general(
            kaug[...], qaug[p * chunk_rows : (p + 1) * chunk_rows], NT, preferred_element_type=jnp.float32
        )
        top = jnp.max(s, axis=0, keepdims=True) * scale2
        total = jnp.sum(jnp.exp2(s * scale2 - top), axis=0, keepdims=True)
        lse[pl.ds(v * per + p, 1), :] = top + jnp.log2(total)

    @pl.when(v == pl.num_programs(0) - 1)
    def _():
        everything = lse[...]
        for i in range(out_ref.shape[0]):
            out_ref[i] = everything


def to_column(row):
    r = lax.broadcasted_iota(jnp.int32, (128, 128), 0)
    c = lax.broadcasted_iota(jnp.int32, (128, 128), 1)
    return jnp.sum(jnp.where(r == c, row, 0.0), axis=1, keepdims=True)


def columns_kernel(
    first_ref, q_ref, k_ref, next_ref, prev_ref, lim_ref, parts_ref, width_ref, out_ref,
    kaug, qaug, lse, cols, *, heads, row_count, scale2, key_total,
):
    v = pl.program_id(0)
    per, chunk_rows, head_dim = q_ref.shape
    key_dev = k_ref.shape[0]
    block = 256

    @pl.when(v == 0)
    def _():
        for b in range(key_dev // block):
            kaug[b * block : (b + 1) * block, head_dim:] = penalty_rows(
                first_ref[0] + b * block, block, lim_ref[...], False, 0, 0
            )
        kaug[key_dev:, head_dim:] = penalty_rows(first_ref[0], HALO, lim_ref[...], True, key_total, key_dev)
        kaug[key_dev:, :head_dim] = jnp.zeros((HALO, head_dim), jnp.bfloat16)
        hot = one_hot_rows(chunk_rows, heads, row_count)
        for p in range(per):
            qaug[p * chunk_rows : (p + 1) * chunk_rows, head_dim:] = hot
        peers = parts_ref.shape[0]
        top = parts_ref[0]
        for i in range(1, peers):
            top = jnp.maximum(top, parts_ref[i])
        total = jnp.exp2(parts_ref[0] - top)
        for i in range(1, peers):
            total = total + jnp.exp2(parts_ref[i] - top)
        lse[...] = top + jnp.log2(total)

    kaug[:key_dev, :head_dim] = k_ref[...]
    kaug[key_dev : key_dev + EDGE, :head_dim] = next_ref[...]
    kaug[key_dev + HALO - EDGE :, :head_dim] = prev_ref[...]
    for p in range(per):
        qaug[p * chunk_rows : (p + 1) * chunk_rows, :head_dim] = q_ref[p]
    columns = []
    for p in range(per):
        row = lse[pl.ds(v * per + p, 1), :]
        for j in range(chunk_rows // 128):
            columns.append(to_column(row[:, j * 128 : (j + 1) * 128]))
    shift = jnp.concatenate(columns, axis=0)
    start = 0
    while start < key_dev + HALO:
        size = min(block, key_dev + HALO - start)
        s = lax.dot_general(qaug[...], kaug[start : start + size], NT, preferred_element_type=jnp.float32)
        weights = jnp.exp2(s * scale2 - shift)
        cols[v, :, start : start + size] = jnp.sum(weights.reshape(-1, 8, size), axis=0)
        start += size

    @pl.when(v == pl.num_programs(0) - 1)
    def _():
        width = width_ref[...]
        below = width // 2
        above = (width - 1) // 2
        whole = jnp.sum(cols[...], axis=1)
        length = whole.shape[1]
        pooled = jnp.where(above >= 0, whole, 0.0)
        for tap in range(1, RAD + 1):
            pooled = pooled + jnp.where(tap <= above, pltpu.roll(whole, length - tap, 1), 0.0)
            pooled = pooled + jnp.where(tap <= below, pltpu.roll(whole, tap, 1), 0.0)
        pooled = pooled / width.astype(jnp.float32)
        piece = key_dev // out_ref.shape[0]
        for i in range(out_ref.shape[0]):
            out_ref[i] = pooled[:, i * piece : (i + 1) * piece]


def row_stats(first, chunks, keys, lim, key_heads, heads, scale2):
    n, chunk_rows, head_dim = chunks.shape
    per = n // key_heads
    key_dev = keys.shape[0]
    return pl.pallas_call(
        lambda *refs: stats_kernel(*refs, heads=heads, row_count=chunk_rows // heads, scale2=scale2),
        out_shape=jax.ShapeDtypeStruct((n, n, chunk_rows), jnp.float32),
        grid=(key_heads,),
        in_specs=[
            pl.BlockSpec(memory_space=pltpu.SMEM),
            pl.BlockSpec((per, chunk_rows, head_dim), lambda v: (v, 0, 0)),
            pl.BlockSpec((key_dev, head_dim), lambda v: (0, v)),
            pl.BlockSpec((1, 128), lambda v: (0, 0)),
        ],
        out_specs=pl.BlockSpec((n, n, chunk_rows), lambda v: (0, 0, 0)),
        scratch_shapes=[
            pltpu.VMEM((key_dev, 2 * head_dim), jnp.bfloat16),
            pltpu.VMEM((per * chunk_rows, 2 * head_dim), jnp.bfloat16),
            pltpu.VMEM((n, chunk_rows), jnp.float32),
        ],
        name="row_stats",
    )(first, chunks, keys, lim)


def key_columns(first, chunks, keys, after, before, lim, parts, width, key_heads, heads, scale2, key_total, owners):
    n, chunk_rows, head_dim = chunks.shape
    per = n // key_heads
    key_dev = keys.shape[0]
    return pl.pallas_call(
        lambda *refs: columns_kernel(
            *refs, heads=heads, row_count=chunk_rows // heads, scale2=scale2, key_total=key_total
        ),
        out_shape=jax.ShapeDtypeStruct((owners, key_heads, key_dev // owners), jnp.float32),
        grid=(key_heads,),
        in_specs=[
            pl.BlockSpec(memory_space=pltpu.SMEM),
            pl.BlockSpec((per, chunk_rows, head_dim), lambda v: (v, 0, 0)),
            pl.BlockSpec((key_dev, head_dim), lambda v: (0, v)),
            pl.BlockSpec((EDGE, head_dim), lambda v: (0, v)),
            pl.BlockSpec((EDGE, head_dim), lambda v: (0, v)),
            pl.BlockSpec((1, 128), lambda v: (0, 0)),
            pl.BlockSpec((n, n, chunk_rows), lambda v: (0, 0, 0)),
            pl.BlockSpec((key_heads, 1), lambda v: (0, 0)),
        ],
        out_specs=pl.BlockSpec((owners, key_heads, key_dev // owners), lambda v: (0, 0, 0)),
        scratch_shapes=[
            pltpu.VMEM((key_dev + HALO, 2 * head_dim), jnp.bfloat16),
            pltpu.VMEM((per * chunk_rows, 2 * head_dim), jnp.bfloat16),
            pltpu.VMEM((n, chunk_rows), jnp.float32),
            pltpu.VMEM((key_heads, 8, key_dev + HALO), jnp.float32),
        ],
        name="key_columns",
    )(first, chunks, keys, after, before, lim, parts, width)


def sent_to_all(array, axis):
    length = lax.axis_size(axis)
    return lax.all_to_all(jnp.broadcast_to(array[None], (length, *array.shape)), axis, 0, 0, tiled=True)


def per_device(queries, prefix_keys, lengths, positions, pool_width, scorer_in, scorer_out):
    row_count, heads, head_dim = queries.shape
    key_heads = pool_width.shape[0]
    key_dev = prefix_keys.shape[0]
    shards = lax.axis_size("ctx")
    owners = lax.axis_size("req")
    scale2 = LOG2E / math.sqrt(head_dim)
    limits = jnp.minimum(positions, lengths[:, None] - 1).reshape(1, row_count)
    lim = jnp.pad(limits, ((0, 0), (0, 128 - row_count)), constant_values=2**30)
    first = (lax.axis_index("ctx") * key_dev).reshape(1).astype(jnp.int32)
    up = [(i, i + 1) for i in range(shards - 1)]
    chunks = sent_to_all(queries.reshape(row_count * heads, head_dim), "ctx")
    chunks = chunks.reshape(shards, row_count * heads, head_dim)
    before = lax.ppermute(prefix_keys[key_dev - EDGE :], "ctx", up)
    after = lax.ppermute(prefix_keys[:EDGE], "ctx", [(b, a) for a, b in up])

    owned = key_dev // owners
    owned_keys = lax.dynamic_slice_in_dim(prefix_keys, lax.axis_index("req") * owned, owned, 0)
    hidden = jax.nn.silu(jnp.dot(owned_keys, scorer_in, preferred_element_type=jnp.float32)).astype(jnp.bfloat16)
    gating = jnp.dot(hidden, scorer_out, preferred_element_type=jnp.float32)
    gate = (2.0 * jax.nn.sigmoid(gating)).T
    chunks, gate, before, after = lax.optimization_barrier((chunks, gate, before, after))

    local = row_stats(first, chunks, prefix_keys, lim, key_heads, heads, scale2)
    parts = lax.all_to_all(local, "ctx", 0, 0, tiled=True)
    pooled = key_columns(
        first, chunks, prefix_keys, after, before, lim, parts, pool_width.reshape(key_heads, 1),
        key_heads, heads, scale2, shards * key_dev, owners,
    )
    pieces = lax.all_to_all(pooled, "req", 0, 0, tiled=True)
    return jnp.sum(pieces, axis=0) * gate


def solution(mesh):
    placed = (P("req", "ctx", None), P("ctx", None), P("req"), P("req", None), P(), P(), P())
    return jax.shard_map(
        per_device, mesh=mesh, in_specs=placed, out_specs=P(None, ("ctx", "req")), check_vma=False
    )
```

```python
import math

import jax
import jax.numpy as jnp
from jax import lax
from jax.experimental import pallas as pl
from jax.experimental.pallas import tpu as pltpu
from jax.sharding import PartitionSpec as P


RAD = 3
MASKED = -1e30
LOG2E = 1.4426950408889634
HALO = 128
EDGE = 16
HEADS_STEP = 2
SAMPLE = 64
LARGE = 2.0**100
NT = (((1,), (1,)), ((), ()))


def penalty_rows(first_key, count, limits, is_halo, key_total, key_dev):
    local = lax.broadcasted_iota(jnp.int32, (count, 128), 0)
    if is_halo:
        after = local < HALO // 2
        key = jnp.where(after, first_key + key_dev + local, first_key - HALO + local)
        real = ((local < RAD) | (local >= HALO - RAD)) & (key >= 0) & (key < key_total)
        return jnp.where(real & (key <= limits), 0.0, MASKED).astype(jnp.bfloat16)
    return jnp.where(first_key + local <= limits, 0.0, MASKED).astype(jnp.bfloat16)


def one_hot_rows(chunk_rows, heads):
    row = lax.broadcasted_iota(jnp.int32, (chunk_rows, 128), 0)
    lane = lax.broadcasted_iota(jnp.int32, (chunk_rows, 128), 1)
    low = lane * heads
    return jnp.where((row >= low) & (row < low + heads), 1.0, 0.0).astype(jnp.bfloat16)


def stats_kernel(first_ref, q_ref, k_ref, lim_ref, out_ref, pen, hot, lse, totals, *, heads, scale2):
    step = pl.program_id(0)
    group, chunk_rows, head_dim = q_ref.shape
    key_dev = k_ref.shape[0]
    per = group * head_dim // k_ref.shape[1]
    block = 256

    @pl.when(step == 0)
    def _():
        for b in range(key_dev // block):
            pen[b * block : (b + 1) * block] = penalty_rows(
                first_ref[0] + b * block, block, lim_ref[...], False, 0, 0
            )
        hot[...] = one_hot_rows(chunk_rows, heads)

    def scored(chunk):
        v = chunk // per
        keys = jnp.concatenate([k_ref[:, v * head_dim : (v + 1) * head_dim], pen[...]], axis=1)
        rows = jnp.concatenate([q_ref[chunk], hot[...]], axis=1)
        return lax.dot_general(keys, rows, NT, preferred_element_type=jnp.float32)

    for chunk in range(group):
        s = scored(chunk)
        base = jnp.max(s[:SAMPLE], axis=0, keepdims=True)
        total = jnp.sum(jnp.exp2((s - base) * scale2), axis=0, keepdims=True)
        lse[pl.ds(step * group + chunk, 1), :] = base * scale2 + jnp.log2(total)
        totals[chunk : chunk + 1] = total

    @pl.when(jnp.logical_not(jnp.max(totals[...]) < LARGE))
    def _():
        for chunk in range(group):
            s = scored(chunk)
            top = jnp.max(s, axis=0, keepdims=True)
            total = jnp.sum(jnp.exp2((s - top) * scale2), axis=0, keepdims=True)
            lse[pl.ds(step * group + chunk, 1), :] = top * scale2 + jnp.log2(total)

    @pl.when(step == pl.num_programs(0) - 1)
    def _():
        everything = lse[...]
        for i in range(out_ref.shape[0]):
            out_ref[i] = everything


def to_column(row):
    r = lax.broadcasted_iota(jnp.int32, (128, 128), 0)
    c = lax.broadcasted_iota(jnp.int32, (128, 128), 1)
    return jnp.sum(jnp.where(r == c, row, 0.0), axis=1, keepdims=True)


def columns_kernel(
    first_ref, q_ref, k_ref, next_ref, prev_ref, lim_ref, parts_ref, width_ref, out_ref,
    pen, hot, lse, cols, *, heads, scale2, key_total,
):
    step = pl.program_id(0)
    group, chunk_rows, head_dim = q_ref.shape
    key_dev = k_ref.shape[0]
    heads_here = k_ref.shape[1] // head_dim
    per = group // heads_here
    block = 256

    @pl.when(step == 0)
    def _():
        for b in range(key_dev // block):
            pen[b * block : (b + 1) * block] = penalty_rows(
                first_ref[0] + b * block, block, lim_ref[...], False, 0, 0
            )
        pen[key_dev:] = penalty_rows(first_ref[0], HALO, lim_ref[...], True, key_total, key_dev)
        hot[...] = one_hot_rows(chunk_rows, heads)
        peers = parts_ref.shape[0]
        top = parts_ref[0]
        for i in range(1, peers):
            top = jnp.maximum(top, parts_ref[i])
        total = jnp.exp2(parts_ref[0] - top)
        for i in range(1, peers):
            total = total + jnp.exp2(parts_ref[i] - top)
        lse[...] = top + jnp.log2(total)

    for h in range(heads_here):
        lanes = slice(h * head_dim, (h + 1) * head_dim)
        columns = []
        for p in range(per):
            row = lse[pl.ds(step * group + h * per + p, 1), :]
            for j in range(chunk_rows // 128):
                columns.append(to_column(row[:, j * 128 : (j + 1) * 128]))
        shift = jnp.concatenate(columns, axis=0)
        rows = jnp.concatenate(
            [jnp.concatenate([q_ref[h * per + p], hot[...]], axis=1) for p in range(per)], axis=0
        )
        gap = jnp.zeros((HALO - 2 * EDGE, head_dim), jnp.bfloat16)
        edges = jnp.concatenate([next_ref[:, lanes], gap, prev_ref[:, lanes]], axis=0)
        start = 0
        while start < key_dev + HALO:
            size = min(block, key_dev + HALO - start)
            some = edges if start >= key_dev else k_ref[start : start + size, lanes]
            keys = jnp.concatenate([some, pen[start : start + size]], axis=1)
            s = lax.dot_general(rows, keys, NT, preferred_element_type=jnp.float32)
            weights = jnp.exp2(s * scale2 - shift)
            cols[step * heads_here + h, :, start : start + size] = jnp.sum(weights.reshape(-1, 8, size), axis=0)
            start += size

    @pl.when(step == pl.num_programs(0) - 1)
    def _():
        width = width_ref[...]
        below = width // 2
        above = (width - 1) // 2
        whole = jnp.sum(cols[...], axis=1)
        length = whole.shape[1]
        pooled = jnp.where(above >= 0, whole, 0.0)
        for tap in range(1, RAD + 1):
            pooled = pooled + jnp.where(tap <= above, pltpu.roll(whole, length - tap, 1), 0.0)
            pooled = pooled + jnp.where(tap <= below, pltpu.roll(whole, tap, 1), 0.0)
        pooled = pooled / width.astype(jnp.float32)
        piece = key_dev // out_ref.shape[0]
        for i in range(out_ref.shape[0]):
            out_ref[i] = pooled[:, i * piece : (i + 1) * piece]


def row_stats(first, chunks, keys, lim, key_heads, heads, scale2):
    n, chunk_rows, head_dim = chunks.shape
    key_dev = keys.shape[0]
    steps = key_heads // HEADS_STEP
    group = n // steps
    width = HEADS_STEP * head_dim
    return pl.pallas_call(
        lambda *refs: stats_kernel(*refs, heads=heads, scale2=scale2),
        out_shape=jax.ShapeDtypeStruct((n, n, chunk_rows), jnp.float32),
        grid=(steps,),
        in_specs=[
            pl.BlockSpec(memory_space=pltpu.SMEM),
            pl.BlockSpec((group, chunk_rows, head_dim), lambda i: (i, 0, 0)),
            pl.BlockSpec((key_dev, width), lambda i: (0, i)),
            pl.BlockSpec((1, 128), lambda i: (0, 0)),
        ],
        out_specs=pl.BlockSpec((n, n, chunk_rows), lambda i: (0, 0, 0)),
        scratch_shapes=[
            pltpu.VMEM((key_dev, 128), jnp.bfloat16),
            pltpu.VMEM((chunk_rows, 128), jnp.bfloat16),
            pltpu.VMEM((n, chunk_rows), jnp.float32),
            pltpu.VMEM((group, chunk_rows), jnp.float32),
        ],
        name="row_stats",
    )(first, chunks, keys, lim)


def key_columns(first, chunks, keys, after, before, lim, parts, width, key_heads, heads, scale2, key_total, owners):
    n, chunk_rows, head_dim = chunks.shape
    key_dev = keys.shape[0]
    steps = key_heads // HEADS_STEP
    group = n // steps
    wide = HEADS_STEP * head_dim
    return pl.pallas_call(
        lambda *refs: columns_kernel(*refs, heads=heads, scale2=scale2, key_total=key_total),
        out_shape=jax.ShapeDtypeStruct((owners, key_heads, key_dev // owners), jnp.float32),
        grid=(steps,),
        in_specs=[
            pl.BlockSpec(memory_space=pltpu.SMEM),
            pl.BlockSpec((group, chunk_rows, head_dim), lambda i: (i, 0, 0)),
            pl.BlockSpec((key_dev, wide), lambda i: (0, i)),
            pl.BlockSpec((EDGE, wide), lambda i: (0, i)),
            pl.BlockSpec((EDGE, wide), lambda i: (0, i)),
            pl.BlockSpec((1, 128), lambda i: (0, 0)),
            pl.BlockSpec((n, n, chunk_rows), lambda i: (0, 0, 0)),
            pl.BlockSpec((key_heads, 1), lambda i: (0, 0)),
        ],
        out_specs=pl.BlockSpec((owners, key_heads, key_dev // owners), lambda i: (0, 0, 0)),
        scratch_shapes=[
            pltpu.VMEM((key_dev + HALO, 128), jnp.bfloat16),
            pltpu.VMEM((chunk_rows, 128), jnp.bfloat16),
            pltpu.VMEM((n, chunk_rows), jnp.float32),
            pltpu.VMEM((key_heads, 8, key_dev + HALO), jnp.float32),
        ],
        name="key_columns",
    )(first, chunks, keys, after, before, lim, parts, width)


def sent_to_all(array, axis):
    length = lax.axis_size(axis)
    return lax.all_to_all(jnp.broadcast_to(array[None], (length, *array.shape)), axis, 0, 0, tiled=True)


def per_device(queries, prefix_keys, lengths, positions, pool_width, scorer_in, scorer_out):
    row_count, heads, head_dim = queries.shape
    key_heads = pool_width.shape[0]
    key_dev = prefix_keys.shape[0]
    shards = lax.axis_size("ctx")
    owners = lax.axis_size("req")
    scale2 = LOG2E / math.sqrt(head_dim)
    limits = jnp.minimum(positions, lengths[:, None] - 1).reshape(1, row_count)
    lim = jnp.pad(limits, ((0, 0), (0, 128 - row_count)), constant_values=2**30)
    first = (lax.axis_index("ctx") * key_dev).reshape(1).astype(jnp.int32)
    up = [(i, i + 1) for i in range(shards - 1)]
    chunks = sent_to_all(queries.reshape(row_count * heads, head_dim), "ctx")
    chunks = chunks.reshape(shards, row_count * heads, head_dim)
    before = lax.ppermute(prefix_keys[key_dev - EDGE :], "ctx", up)
    after = lax.ppermute(prefix_keys[:EDGE], "ctx", [(b, a) for a, b in up])

    owned = key_dev // owners
    owned_keys = lax.dynamic_slice_in_dim(prefix_keys, lax.axis_index("req") * owned, owned, 0)
    hidden = jax.nn.silu(jnp.dot(owned_keys, scorer_in, preferred_element_type=jnp.float32)).astype(jnp.bfloat16)
    gating = jnp.dot(hidden, scorer_out, preferred_element_type=jnp.float32)
    gate = (2.0 * jax.nn.sigmoid(gating)).T
    chunks, gate = lax.optimization_barrier((chunks, gate))
    chunks = pltpu.with_memory_space_constraint(chunks, pltpu.VMEM)

    local = row_stats(first, chunks, prefix_keys, lim, key_heads, heads, scale2)
    parts = lax.all_to_all(local, "ctx", 0, 0, tiled=True)
    parts = pltpu.with_memory_space_constraint(parts, pltpu.VMEM)
    pooled = key_columns(
        first, chunks, prefix_keys, after, before, lim, parts, pool_width.reshape(key_heads, 1),
        key_heads, heads, scale2, shards * key_dev, owners,
    )
    pieces = lax.all_to_all(pooled, "req", 0, 0, tiled=True)
    return jnp.sum(pieces, axis=0) * gate


def solution(mesh):
    placed = (P("req", "ctx", None), P("ctx", None), P("req"), P("req", None), P(), P(), P())

    return jax.shard_map(per_device, mesh=mesh, in_specs=placed, out_specs=P(None, ("ctx", "req")), check_vma=False)
```

```python
import math

import jax
import jax.numpy as jnp
from jax import lax
from jax.experimental import pallas as pl
from jax.experimental.pallas import tpu as pltpu
from jax.sharding import PartitionSpec as P


RAD = 3
MASKED = -1e30
LOG2E = 1.4426950408889634
HALO = 128
EDGE = 16
HEADS_STEP = 2
SAMPLE = 16
LARGE = 2.0**100
NT = (((1,), (1,)), ((), ()))


def penalty_rows(first_key, count, limits, is_halo, key_total, key_dev):
    local = lax.broadcasted_iota(jnp.int32, (count, 128), 0)
    if is_halo:
        after = local < HALO // 2
        key = jnp.where(after, first_key + key_dev + local, first_key - HALO + local)
        real = ((local < RAD) | (local >= HALO - RAD)) & (key >= 0) & (key < key_total)
        return jnp.where(real & (key <= limits), 0.0, MASKED).astype(jnp.bfloat16)
    return jnp.where(first_key + local <= limits, 0.0, MASKED).astype(jnp.bfloat16)


def one_hot_rows(chunk_rows, heads):
    row = lax.broadcasted_iota(jnp.int32, (chunk_rows, 128), 0)
    lane = lax.broadcasted_iota(jnp.int32, (chunk_rows, 128), 1)
    low = lane * heads
    return jnp.where((row >= low) & (row < low + heads), 1.0, 0.0).astype(jnp.bfloat16)


def masks_kernel(first_ref, lim_ref, pen_ref, hot_ref, *, heads, key_dev, key_total):
    block = 256
    for start in range(0, key_dev, block):
        pen_ref[start : start + block] = penalty_rows(first_ref[0] + start, block, lim_ref[...], False, 0, 0)
    pen_ref[key_dev:] = penalty_rows(first_ref[0], HALO, lim_ref[...], True, key_total, key_dev)
    hot_ref[...] = one_hot_rows(hot_ref.shape[0], heads)


def stats_kernel(
    q_ref, k_ref, pen, hot, keys_ref, out_ref, lse, totals, spare, arrival, *, scale2, group
):
    step = pl.program_id(0)
    _, head_dim = q_ref.shape[1:]
    key_dev = k_ref.shape[0]
    per = group * head_dim // k_ref.shape[1]

    def scored(keys, chunk):
        keys = jnp.concatenate([keys, pen[:key_dev]], axis=1)
        rows = jnp.concatenate([q_ref[chunk], hot[...]], axis=1)
        return lax.dot_general(keys, rows, NT, preferred_element_type=jnp.float32)

    def finish(s, base, chunk):
        total = jnp.sum(jnp.exp2((s - base) * scale2), axis=0, keepdims=True)
        lse[pl.ds(chunk, 1), :] = base * scale2 + jnp.log2(total)
        return total

    for i in range(group):
        v = i // per
        chunk = step * group + i
        s = scored(k_ref[:, v * head_dim : (v + 1) * head_dim], chunk)
        base = jnp.max(s[:SAMPLE], axis=0, keepdims=True)
        totals[pl.ds(chunk, 1), :] = finish(s, base, chunk)

    @pl.when(step == pl.num_programs(0) - 1)
    def _():
        @pl.when(jnp.logical_not(jnp.max(totals[...]) < LARGE))
        def _():
            def redo(v, carry):
                start = pl.multiple_of(v * head_dim, head_dim)
                move = pltpu.make_async_copy(keys_ref.at[:, pl.ds(start, head_dim)], spare, arrival)
                move.start()
                move.wait()
                for p in range(per):
                    s = scored(spare[...], v * per + p)
                    finish(s, jnp.max(s, axis=0, keepdims=True), v * per + p)
                return carry

            lax.fori_loop(0, q_ref.shape[0] // per, redo, 0)

        everything = lse[...]
        for i in range(out_ref.shape[0]):
            out_ref[i] = everything


def to_column(row):
    r = lax.broadcasted_iota(jnp.int32, (128, 128), 0)
    c = lax.broadcasted_iota(jnp.int32, (128, 128), 1)
    return jnp.sum(jnp.where(r == c, row, 0.0), axis=1, keepdims=True)


def columns_kernel(
    width_ref, q_ref, k_ref, pen, hot, next_ref, prev_ref, parts_ref, out_ref, lse, cols, *, scale2
):
    step = pl.program_id(0)
    group, chunk_rows, head_dim = q_ref.shape
    key_dev = k_ref.shape[0]
    heads_here = k_ref.shape[1] // head_dim
    per = group // heads_here
    block = 256

    @pl.when(step == 0)
    def _():
        peers = parts_ref.shape[0]
        top = parts_ref[0]
        for i in range(1, peers):
            top = jnp.maximum(top, parts_ref[i])
        total = jnp.exp2(parts_ref[0] - top)
        for i in range(1, peers):
            total = total + jnp.exp2(parts_ref[i] - top)
        lse[...] = top + jnp.log2(total)

    for h in range(heads_here):
        lanes = slice(h * head_dim, (h + 1) * head_dim)
        columns = []
        for p in range(per):
            row = lse[pl.ds(step * group + h * per + p, 1), :]
            for j in range(chunk_rows // 128):
                columns.append(to_column(row[:, j * 128 : (j + 1) * 128]))
        shift = jnp.concatenate(columns, axis=0)
        rows = jnp.concatenate(
            [jnp.concatenate([q_ref[h * per + p], hot[...]], axis=1) for p in range(per)], axis=0
        )
        gap = jnp.zeros((HALO - 2 * EDGE, head_dim), jnp.bfloat16)
        edges = jnp.concatenate([next_ref[:, lanes], gap, prev_ref[:, lanes]], axis=0)
        start = 0
        while start < key_dev + HALO:
            size = min(block, key_dev + HALO - start)
            some = edges if start >= key_dev else k_ref[start : start + size, lanes]
            keys = jnp.concatenate([some, pen[start : start + size]], axis=1)
            s = lax.dot_general(rows, keys, NT, preferred_element_type=jnp.float32)
            weights = jnp.exp2(s * scale2 - shift)
            total = jnp.sum(weights, axis=0, keepdims=True)
            here = lax.broadcasted_iota(jnp.int32, (cols.shape[0], size), 0) == step * heads_here + h
            cols[:, start : start + size] = jnp.where(here, total, cols[:, start : start + size])
            start += size

    @pl.when(step == pl.num_programs(0) - 1)
    def _():
        head = lax.broadcasted_iota(jnp.int32, (cols.shape[0], 1), 0)
        width = jnp.zeros_like(head)
        for v in range(cols.shape[0]):
            width = jnp.where(head == v, width_ref[v], width)
        below = width // 2
        above = (width - 1) // 2
        whole = cols[...]
        length = whole.shape[1]
        pooled = jnp.where(above >= 0, whole, 0.0)
        for tap in range(1, RAD + 1):
            pooled = pooled + jnp.where(tap <= above, pltpu.roll(whole, length - tap, 1), 0.0)
            pooled = pooled + jnp.where(tap <= below, pltpu.roll(whole, tap, 1), 0.0)
        pooled = pooled / width.astype(jnp.float32)
        piece = key_dev // out_ref.shape[0]
        for i in range(out_ref.shape[0]):
            out_ref[i] = pooled[:, i * piece : (i + 1) * piece]


def key_masks(first, lim, chunk_rows, heads, key_dev, key_total):
    whole = pl.BlockSpec(memory_space=pltpu.VMEM)
    return pl.pallas_call(
        lambda *refs: masks_kernel(*refs, heads=heads, key_dev=key_dev, key_total=key_total),
        out_shape=(
            pltpu.VMEM((key_dev + HALO, 128), jnp.bfloat16),
            pltpu.VMEM((chunk_rows, 128), jnp.bfloat16),
        ),
        in_specs=[pl.BlockSpec(memory_space=pltpu.SMEM), whole],
        out_specs=(whole, whole),
        name="key_masks",
    )(first, lim)


def row_stats(chunks, keys, pen, hot, key_heads, scale2):
    n, chunk_rows, head_dim = chunks.shape
    key_dev = keys.shape[0]
    steps = key_heads // HEADS_STEP
    group = n // steps
    width = HEADS_STEP * head_dim
    return pl.pallas_call(
        lambda *refs: stats_kernel(*refs, scale2=scale2, group=group),
        out_shape=pltpu.VMEM((n, n, chunk_rows), jnp.float32),
        grid=(steps,),
        in_specs=[
            pl.BlockSpec((n, chunk_rows, head_dim), lambda i: (0, 0, 0)),
            pl.BlockSpec((key_dev, width), lambda i: (0, i)),
            pl.BlockSpec(pen.shape, lambda i: (0, 0)),
            pl.BlockSpec(hot.shape, lambda i: (0, 0)),
            pl.BlockSpec(memory_space=pl.ANY),
        ],
        out_specs=pl.BlockSpec((n, n, chunk_rows), lambda i: (0, 0, 0)),
        scratch_shapes=[
            pltpu.VMEM((n, chunk_rows), jnp.float32),
            pltpu.VMEM((n, chunk_rows), jnp.float32),
            pltpu.VMEM((key_dev, head_dim), jnp.bfloat16),
            pltpu.SemaphoreType.DMA,
        ],
        name="row_stats",
    )(chunks, keys, pen, hot, keys)


def key_columns(width, chunks, keys, pen, hot, after, before, parts, scale2, owners):
    n, chunk_rows, head_dim = chunks.shape
    key_dev = keys.shape[0]
    key_heads = width.shape[0]
    steps = key_heads // HEADS_STEP
    group = n // steps
    wide = HEADS_STEP * head_dim
    return pl.pallas_call(
        lambda *refs: columns_kernel(*refs, scale2=scale2),
        out_shape=pltpu.VMEM((owners, key_heads, key_dev // owners), jnp.float32),
        grid=(steps,),
        in_specs=[
            pl.BlockSpec(memory_space=pltpu.SMEM),
            pl.BlockSpec((group, chunk_rows, head_dim), lambda i: (i, 0, 0)),
            pl.BlockSpec((key_dev, wide), lambda i: (0, i)),
            pl.BlockSpec(pen.shape, lambda i: (0, 0)),
            pl.BlockSpec(hot.shape, lambda i: (0, 0)),
            pl.BlockSpec((EDGE, wide), lambda i: (0, i)),
            pl.BlockSpec((EDGE, wide), lambda i: (0, i)),
            pl.BlockSpec((n, n, chunk_rows), lambda i: (0, 0, 0)),
        ],
        out_specs=pl.BlockSpec((owners, key_heads, key_dev // owners), lambda i: (0, 0, 0)),
        scratch_shapes=[
            pltpu.VMEM((n, chunk_rows), jnp.float32),
            pltpu.VMEM((key_heads, key_dev + HALO), jnp.float32),
        ],
        name="key_columns",
    )(width, chunks, keys, pen, hot, after, before, parts)


def copies_kernel(x_ref, out_ref, arrivals):
    moves = [
        pltpu.make_async_copy(x_ref, out_ref.at[i], arrivals.at[i]) for i in range(out_ref.shape[0])
    ]
    for move in moves:
        move.start()
    for move in moves:
        move.wait()


def sent_to_all(array, axis):
    length = lax.axis_size(axis)
    copies = pl.pallas_call(
        copies_kernel,
        out_shape=jax.ShapeDtypeStruct((length, *array.shape), array.dtype),
        in_specs=[pl.BlockSpec(memory_space=pltpu.VMEM)],
        out_specs=pl.BlockSpec(memory_space=pl.ANY),
        scratch_shapes=[pltpu.SemaphoreType.DMA((length,))],
        name="copies",
    )(array)
    return lax.all_to_all(copies, axis, 0, 0, tiled=True)


def per_device(queries, prefix_keys, lengths, positions, pool_width, scorer_in, scorer_out):
    row_count, heads, head_dim = queries.shape
    key_heads = pool_width.shape[0]
    key_dev = prefix_keys.shape[0]
    shards = lax.axis_size("ctx")
    owners = lax.axis_size("req")
    scale2 = LOG2E / math.sqrt(head_dim)
    limits = jnp.minimum(positions, lengths[:, None] - 1).reshape(1, row_count)
    lim = jnp.pad(limits, ((0, 0), (0, 128 - row_count)), constant_values=2**30)
    first = (lax.axis_index("ctx") * key_dev).reshape(1).astype(jnp.int32)
    up = [(i, i + 1) for i in range(shards - 1)]
    chunks = sent_to_all(queries.reshape(row_count * heads, head_dim), "ctx")
    chunks = chunks.reshape(shards, row_count * heads, head_dim)
    before = lax.ppermute(prefix_keys[key_dev - EDGE :], "ctx", up)
    after = lax.ppermute(prefix_keys[:EDGE], "ctx", [(b, a) for a, b in up])

    owned = key_dev // owners
    owned_keys = lax.dynamic_slice_in_dim(prefix_keys, lax.axis_index("req") * owned, owned, 0)
    hidden = jax.nn.silu(jnp.dot(owned_keys, scorer_in, preferred_element_type=jnp.float32)).astype(jnp.bfloat16)
    gating = jnp.dot(hidden, scorer_out, preferred_element_type=jnp.float32)
    gate = (2.0 * jax.nn.sigmoid(gating)).T
    pen, hot = key_masks(first, lim, row_count * heads, heads, key_dev, shards * key_dev)
    chunks, gate = lax.optimization_barrier((chunks, gate))
    chunks, pen, hot, after, before = (
        pltpu.with_memory_space_constraint(x, pltpu.VMEM) for x in (chunks, pen, hot, after, before)
    )
    local = row_stats(chunks, prefix_keys, pen, hot, key_heads, scale2)
    parts = lax.all_to_all(local, "ctx", 0, 0, tiled=True)
    parts = pltpu.with_memory_space_constraint(parts, pltpu.VMEM)
    pooled = key_columns(pool_width, chunks, prefix_keys, pen, hot, after, before, parts, scale2, owners)
    pieces = lax.all_to_all(pooled, "req", 0, 0, tiled=True)
    return jnp.sum(pieces, axis=0) * gate


def solution(mesh):
    placed = (P("req", "ctx", None), P("ctx", None), P("req"), P("req", None), P(), P(), P())

    return jax.shard_map(
        per_device, mesh=mesh, in_specs=placed, out_specs=P(None, ("ctx", "req")), check_vma=False
    )
```

```python
import math

import jax
import jax.numpy as jnp
from jax import lax
from jax.experimental import pallas as pl
from jax.experimental.pallas import tpu as pltpu
from jax.sharding import PartitionSpec as P


RAD = 3
MASKED = -1e30
LOG2E = 1.4426950408889634
HALO = 128
EDGE = 16
HEADS_STEP = 2
SAMPLE = 16
PART = 4
LARGE = 2.0**100
NT = (((1,), (1,)), ((), ()))


def penalty_rows(first_key, count, limits, is_halo, key_total, key_dev):
    local = lax.broadcasted_iota(jnp.int32, (count, 128), 0)
    if is_halo:
        after = local < HALO // 2
        key = jnp.where(after, first_key + key_dev + local, first_key - HALO + local)
        real = ((local < RAD) | (local >= HALO - RAD)) & (key >= 0) & (key < key_total)
        return jnp.where(real & (key <= limits), 0.0, MASKED).astype(jnp.bfloat16)
    return jnp.where(first_key + local <= limits, 0.0, MASKED).astype(jnp.bfloat16)


def one_hot_rows(chunk_rows, heads):
    row = lax.broadcasted_iota(jnp.int32, (chunk_rows, 128), 0)
    lane = lax.broadcasted_iota(jnp.int32, (chunk_rows, 128), 1)
    low = lane * heads
    return jnp.where((row >= low) & (row < low + heads), 1.0, 0.0).astype(jnp.bfloat16)


def masks_kernel(first_ref, lim_ref, pen_ref, hot_ref, *, heads, key_dev, key_total):
    block = 256
    for start in range(0, key_dev, block):
        pen_ref[start : start + block] = penalty_rows(first_ref[0] + start, block, lim_ref[...], False, 0, 0)
    pen_ref[key_dev:] = penalty_rows(first_ref[0], HALO, lim_ref[...], True, key_total, key_dev)
    hot_ref[...] = one_hot_rows(hot_ref.shape[0], heads)


def stats_kernel(
    q_ref, k_ref, pen, hot, keys_ref, out_ref, lse, totals, spare, arrival, *, scale2, group
):
    step = pl.program_id(0)
    _, head_dim = q_ref.shape[1:]
    key_dev = k_ref.shape[0]
    per = group * head_dim // k_ref.shape[1]

    def scored(keys, chunk):
        keys = jnp.concatenate([keys, pen[:key_dev]], axis=1)
        rows = jnp.concatenate([q_ref[chunk], hot[...]], axis=1)
        return lax.dot_general(keys, rows, NT, preferred_element_type=jnp.float32)

    def finish(s, base, chunk):
        total = jnp.sum(jnp.exp2((s - base) * scale2), axis=0, keepdims=True)
        lse[pl.ds(chunk, 1), :] = base * scale2 + jnp.log2(total)
        return total

    for i in range(group):
        v = i // per
        chunk = step * group + i
        s = scored(k_ref[:, v * head_dim : (v + 1) * head_dim], chunk)
        base = jnp.max(s[:SAMPLE], axis=0, keepdims=True)
        totals[pl.ds(chunk, 1), :] = finish(s, base, chunk)

    @pl.when(step == pl.num_programs(0) - 1)
    def _():
        @pl.when(jnp.logical_not(jnp.max(totals[...]) < LARGE))
        def _():
            def redo(v, carry):
                start = pl.multiple_of(v * head_dim, head_dim)
                move = pltpu.make_async_copy(keys_ref.at[:, pl.ds(start, head_dim)], spare, arrival)
                move.start()
                move.wait()
                for p in range(per):
                    s = scored(spare[...], v * per + p)
                    finish(s, jnp.max(s, axis=0, keepdims=True), v * per + p)
                return carry

            lax.fori_loop(0, q_ref.shape[0] // per, redo, 0)

        everything = lse[...]
        for i in range(out_ref.shape[0]):
            out_ref[i] = everything


def to_column(row):
    r = lax.broadcasted_iota(jnp.int32, (128, 128), 0)
    c = lax.broadcasted_iota(jnp.int32, (128, 128), 1)
    return jnp.sum(jnp.where(r == c, row, 0.0), axis=1, keepdims=True)


def columns_kernel(
    width_ref, q_ref, k_ref, pen, hot, next_ref, prev_ref, parts_ref, out_ref, lse, cols, *, scale2
):
    step = pl.program_id(0)
    n, chunk_rows, head_dim = q_ref.shape
    key_dev = k_ref.shape[0]
    heads_here = k_ref.shape[1] // head_dim
    per = n // cols.shape[0]
    group = heads_here * per
    block = 256

    @pl.when(step == 0)
    def _():
        peers = parts_ref.shape[0]
        top = parts_ref[0]
        for i in range(1, peers):
            top = jnp.maximum(top, parts_ref[i])
        total = jnp.exp2(parts_ref[0] - top)
        for i in range(1, peers):
            total = total + jnp.exp2(parts_ref[i] - top)
        lse[...] = top + jnp.log2(total)

    for h in range(heads_here):
        lanes = slice(h * head_dim, (h + 1) * head_dim)
        columns = []
        for p in range(per):
            row = lse[pl.ds(step * group + h * per + p, 1), :]
            for j in range(chunk_rows // 128):
                columns.append(to_column(row[:, j * 128 : (j + 1) * 128]))
        shift = jnp.concatenate(columns, axis=0)
        rows = jnp.concatenate(
            [jnp.concatenate([q_ref[step * group + h * per + p], hot[...]], axis=1) for p in range(per)], axis=0
        )
        gap = jnp.zeros((HALO - 2 * EDGE, head_dim), jnp.bfloat16)
        edges = jnp.concatenate([next_ref[:, lanes], gap, prev_ref[:, lanes]], axis=0)
        start = 0
        while start < key_dev + HALO:
            size = min(block, key_dev + HALO - start)
            some = edges if start >= key_dev else k_ref[start : start + size, lanes]
            keys = jnp.concatenate([some, pen[start : start + size]], axis=1)
            s = lax.dot_general(rows, keys, NT, preferred_element_type=jnp.float32)
            weights = jnp.exp2(s * scale2 - shift)
            total = jnp.sum(weights, axis=0, keepdims=True)
            here = lax.broadcasted_iota(jnp.int32, (cols.shape[0], size), 0) == step * heads_here + h
            cols[:, start : start + size] = jnp.where(here, total, cols[:, start : start + size])
            start += size

    @pl.when(step == pl.num_programs(0) - 1)
    def _():
        head = lax.broadcasted_iota(jnp.int32, (cols.shape[0], 1), 0)
        width = jnp.zeros_like(head)
        for v in range(cols.shape[0]):
            width = jnp.where(head == v, width_ref[v], width)
        below = width // 2
        above = (width - 1) // 2
        whole = cols[...]
        length = whole.shape[1]
        pooled = jnp.where(above >= 0, whole, 0.0)
        for tap in range(1, RAD + 1):
            pooled = pooled + jnp.where(tap <= above, pltpu.roll(whole, length - tap, 1), 0.0)
            pooled = pooled + jnp.where(tap <= below, pltpu.roll(whole, tap, 1), 0.0)
        pooled = pooled / width.astype(jnp.float32)
        piece = key_dev // out_ref.shape[0]
        for i in range(out_ref.shape[0]):
            out_ref[i] = pooled[:, i * piece : (i + 1) * piece]


def key_masks(first, lim, chunk_rows, heads, key_dev, key_total):
    whole = pl.BlockSpec(memory_space=pltpu.VMEM)
    return pl.pallas_call(
        lambda *refs: masks_kernel(*refs, heads=heads, key_dev=key_dev, key_total=key_total),
        out_shape=(
            pltpu.VMEM((key_dev + HALO, 128), jnp.bfloat16),
            pltpu.VMEM((chunk_rows, 128), jnp.bfloat16),
        ),
        in_specs=[pl.BlockSpec(memory_space=pltpu.SMEM), whole],
        out_specs=(whole, whole),
        name="key_masks",
    )(first, lim)


def row_stats(chunks, keys, pen, hot, key_heads, scale2):
    n, chunk_rows, head_dim = chunks.shape
    key_dev = keys.shape[0]
    steps = key_heads // HEADS_STEP
    group = n // steps
    width = HEADS_STEP * head_dim
    whole = pl.BlockSpec(memory_space=pltpu.VMEM)
    return pl.pallas_call(
        lambda *refs: stats_kernel(*refs, scale2=scale2, group=group),
        out_shape=pltpu.VMEM((n, n, chunk_rows), jnp.float32),
        grid=(steps,),
        in_specs=[
            whole,
            pl.BlockSpec((key_dev, width), lambda i: (0, i)),
            whole,
            whole,
            pl.BlockSpec(memory_space=pl.ANY),
        ],
        out_specs=whole,
        scratch_shapes=[
            pltpu.VMEM((n, chunk_rows), jnp.float32),
            pltpu.VMEM((n, chunk_rows), jnp.float32),
            pltpu.VMEM((key_dev, head_dim), jnp.bfloat16),
            pltpu.SemaphoreType.DMA,
        ],
        name="row_stats",
    )(chunks, keys, pen, hot, keys)


def key_columns(width, chunks, keys, pen, hot, after, before, parts, scale2, owners):
    n, chunk_rows, head_dim = chunks.shape
    key_dev = keys.shape[0]
    key_heads = width.shape[0]
    steps = key_heads // HEADS_STEP
    wide = HEADS_STEP * head_dim
    whole = pl.BlockSpec(memory_space=pltpu.VMEM)
    return pl.pallas_call(
        lambda *refs: columns_kernel(*refs, scale2=scale2),
        out_shape=pltpu.VMEM((owners, key_heads, key_dev // owners), jnp.float32),
        grid=(steps,),
        in_specs=[
            pl.BlockSpec(memory_space=pltpu.SMEM),
            whole,
            pl.BlockSpec((key_dev, wide), lambda i: (0, i)),
            whole,
            whole,
            pl.BlockSpec((EDGE, wide), lambda i: (0, i)),
            pl.BlockSpec((EDGE, wide), lambda i: (0, i)),
            whole,
        ],
        out_specs=whole,
        scratch_shapes=[
            pltpu.VMEM((n, chunk_rows), jnp.float32),
            pltpu.VMEM((key_heads, key_dev + HALO), jnp.float32),
        ],
        name="key_columns",
    )(width, chunks, keys, pen, hot, after, before, parts)


def copies_kernel(x_ref, out_ref, buffer, arrivals):
    block = x_ref[...]
    count, part = out_ref.shape[0], buffer.shape[0]
    for i in range(part):
        buffer[i] = block
    moves = [
        pltpu.make_async_copy(buffer, out_ref.at[pl.ds(i * part, part)], arrivals.at[i]) for i in range(count // part)
    ]
    for move in moves:
        move.start()
    for move in moves:
        move.wait()


def sent_to_all(array, axis):
    length = lax.axis_size(axis)
    copies = pl.pallas_call(
        copies_kernel,
        out_shape=jax.ShapeDtypeStruct((length, *array.shape), array.dtype),
        in_specs=[pl.BlockSpec(memory_space=pltpu.VMEM)],
        out_specs=pl.BlockSpec(memory_space=pl.ANY),
        scratch_shapes=[pltpu.VMEM((PART, *array.shape), array.dtype), pltpu.SemaphoreType.DMA((length // PART,))],
        name="copies",
    )(array)
    return lax.all_to_all(copies, axis, 0, 0, tiled=True)


def per_device(queries, prefix_keys, lengths, positions, pool_width, scorer_in, scorer_out):
    row_count, heads, head_dim = queries.shape
    key_heads = pool_width.shape[0]
    key_dev = prefix_keys.shape[0]
    shards = lax.axis_size("ctx")
    owners = lax.axis_size("req")
    scale2 = LOG2E / math.sqrt(head_dim)
    limits = jnp.minimum(positions, lengths[:, None] - 1).reshape(1, row_count)
    lim = jnp.pad(limits, ((0, 0), (0, 128 - row_count)), constant_values=2**30)
    first = (lax.axis_index("ctx") * key_dev).reshape(1).astype(jnp.int32)
    up = [(i, i + 1) for i in range(shards - 1)]
    chunks = sent_to_all(queries.reshape(row_count * heads, head_dim), "ctx")
    chunks = chunks.reshape(shards, row_count * heads, head_dim)
    before = lax.ppermute(prefix_keys[key_dev - EDGE :], "ctx", up)
    after = lax.ppermute(prefix_keys[:EDGE], "ctx", [(b, a) for a, b in up])

    owned = key_dev // owners
    owned_keys = lax.dynamic_slice_in_dim(prefix_keys, lax.axis_index("req") * owned, owned, 0)
    hidden = jax.nn.silu(jnp.dot(owned_keys, scorer_in, preferred_element_type=jnp.float32)).astype(jnp.bfloat16)
    gating = jnp.dot(hidden, scorer_out, preferred_element_type=jnp.float32)
    gate = (2.0 * jax.nn.sigmoid(gating)).T
    pen, hot = key_masks(first, lim, row_count * heads, heads, key_dev, shards * key_dev)
    chunks, gate = lax.optimization_barrier((chunks, gate))
    chunks, pen, hot, after, before = (
        pltpu.with_memory_space_constraint(x, pltpu.VMEM) for x in (chunks, pen, hot, after, before)
    )
    local = row_stats(chunks, prefix_keys, pen, hot, key_heads, scale2)
    parts = lax.all_to_all(local, "ctx", 0, 0, tiled=True)
    parts = pltpu.with_memory_space_constraint(parts, pltpu.VMEM)
    pooled = key_columns(pool_width, chunks, prefix_keys, pen, hot, after, before, parts, scale2, owners)
    pieces = lax.all_to_all(pooled, "req", 0, 0, tiled=True)
    return jnp.sum(pieces, axis=0) * gate


def solution(mesh):
    placed = (P("req", "ctx", None), P("ctx", None), P("req"), P("req", None), P(), P(), P())

    return jax.shard_map(per_device, mesh=mesh, in_specs=placed, out_specs=P(None, ("ctx", "req")), check_vma=False)
```
